256 devices in a mesh: group: 8 (over x, core), expert: 8 (over z), hid: 4 (over y).
Axes of the slice: x: 4, y: 4, z: 8, core: 2. Of those that a mesh axis runs over, the one named last changes fastest.
Arguments:
- tokens: bfloat16 [2048, 4096], P(('group', 'expert', 'hid')), may hold values from -6 to 6
- expert_ids: int32 [2048, 2], P(('group', 'expert', 'hid')), may hold values from 0 to 7, all different within a row; in each aligned block of 8 rows (0 to 7, 8 to 15, ...) at most 4 rows name the same one
- gate_numer: int32 [2048, 2], P(('group', 'expert', 'hid')), may hold values from 8 to 64
- gate_weight: bfloat16 [8, 4096, 14336], P('group', None, ('expert', 'hid')), may hold values from -0.09375 to 0.09375
- up_weight: bfloat16 [8, 4096, 14336], P('group', None, ('expert', 'hid')), may hold values from -0.09375 to 0.09375
- down_weight: bfloat16 [8, 14336, 4096], P('group', ('expert', 'hid')), may hold values from -0.046875 to 0.046875
Outputs:
- mixed: bfloat16 [2048, 4096], P(('group', 'expert', 'hid'))
The draws below stay inside these ranges and needn't reach their ends.
Inputs may be any that keep to these rules, and one draw needn't show every extreme that they name: `expert_ids`: A token's 2 ids differ. Within the rows of one device (aligned blocks of 8 rows) no expert is named more than 4 times, and in every draw some block names some expert exactly 4 times.
All inputs are finite; a program needn't handle non-finite values.
Results may differ from the reference program's by a relative error of at most 0.018.
Values may be sent and summed in bfloat16 or wider, within the bound.
No kernel may reach another device: no remote copies, remote signals or barrier semaphores. Data moves between devices by JAX's collectives and lax.ppermute only.
A program may use at most 128 MiB of HBM per device.

```python
import math
import jax
import jax.numpy as jnp
import numpy as np
from jax import lax

D = 4096
FF = 14336
EXPERTS = 8
TOPK = 2
TOK_DEV = 8
CAP = 4
TOKENS = 2048
N_EXPERT = 8
N_HID = 4


def place_ends(values, own_key, smallest, top_value):
    longest = values.shape.index(max(values.shape))
    spots = []
    for shift in (0, 1):
        where = [jax.random.randint(jax.random.fold_in(own_key, axis), (), 0, length) for axis, length in enumerate(values.shape)]
        where[longest] = (where[longest] + shift) % values.shape[longest]
        spots.append(tuple(where))
    return values.at[spots[0]].set(smallest).at[spots[1]].set(top_value)


def level_of(key, extent, cuts, low, high):
    loudness = 1.0
    for position, shards_of in cuts:
        draws = jax.random.uniform(jax.random.fold_in(jax.random.fold_in(key, 6), position), (shards_of,), jnp.float32, low / len(cuts), high / len(cuts))
        loudness = loudness * jnp.repeat(jnp.exp(draws), extent[position] // shards_of).reshape((-1,) + (1,) * (len(extent) - 1 - position))
    return loudness


def shared_out(key, own, number, rows, number_of, top, limit, lean):
    order = jax.random.permutation(key, number_of)
    heavy_load, common = shares(number_of, rows * top, limit, lean, True), shares(number_of, rows * top, limit, lean, False)
    places = jnp.arange(number_of)

    def named(lengths, turn):
        used = int((lengths > 0).sum())
        fixed = max(1, used // 4)
        passed = fixed + (places - fixed + turn * (used - fixed)) % max(1, number_of - fixed)
        return jnp.zeros((number_of,), jnp.int32).at[order[jnp.where(places < fixed, places, passed)]].set(jnp.asarray(lengths, jnp.int32))

    lengths = jnp.where(number % 4 == 0, named(heavy_load, number // 4), named(common, number - number // 4 - 1))
    mixed = jax.random.permutation(jax.random.fold_in(own, 3), number_of)
    donor, taker = mixed[0:number_of // 2 * 2:2], mixed[1:number_of // 2 * 2:2]
    slack = jnp.minimum(lengths[donor] - 1, limit - lengths[taker]) // 2
    slack = jnp.where((donor == order[0]) | (taker == order[0]) | (lengths[taker] == 0), 0, jnp.maximum(slack, 0))
    passed = jax.random.randint(jax.random.fold_in(own, 4), (number_of // 2,), 0, 1 << 20) % (slack + 1)
    lengths = lengths.at[donor].add(-passed).at[taker].add(passed)
    labels = jnp.searchsorted(jnp.cumsum(lengths), jnp.arange(rows * top), side="right").astype(jnp.int32)
    table = labels.reshape(top, rows).T
    table = table[jax.random.permutation(jax.random.fold_in(own, 1), rows)]
    turn = jax.random.randint(jax.random.fold_in(own, 2), (rows, 1), 0, top)
    return jnp.take_along_axis(table, (jnp.arange(top)[None, :] + turn) % top, axis=1)


def shares(count, total, bound, slope, full):
    portions = [(1 << 20) // math.isqrt(standing ** slope) + 1 for standing in range(1, count + 1)]
    largest = bound if full else min(bound, max(-(-total // count), total * portions[0] // sum(portions)))
    least = 1 if total - largest >= count - 1 else 0
    given, rest = [largest] + [least] * (count - 1), total - largest - least * (count - 1)
    while rest > 0:
        movable = [i for i in range(1, count) if given[i] < largest] or [i for i in range(1, count) if given[i] < bound]
        whole, budget = sum([portions[i] for i in movable]), rest
        for i in movable:
            extra = min(bound - given[i], max(1, budget * portions[i] // whole), rest)
            given[i] = given[i] + extra
            rest = rest - extra
    return np.array(given)


def normal_values(rng, shape, scale, limit, shards=(), held_as=jnp.bfloat16):
    array = scale * jax.random.normal(rng, shape, jnp.float32)
    if shards:
        array = array * level_of(rng, shape, shards, -0.22, 0.18)
    return jnp.clip(array, -limit, limit).astype(held_as)


def setup_inputs(seed: int = 0) -> dict:
    arg_keys = jax.random.split(jax.random.key(seed), 7)
    tokens = normal_values(arg_keys[0], (TOKENS, D), 1.0, 6.0, ((0, 256),))
    expert_ids_keys = jax.random.split(jax.random.fold_in(arg_keys[1], 1), TOKENS // TOK_DEV)
    expert_ids_turns = jax.random.permutation(jax.random.fold_in(arg_keys[1], 3), TOKENS // TOK_DEV)
    expert_ids = jax.vmap(lambda own, number: shared_out(jax.random.fold_in(arg_keys[1], 2), own, number, TOK_DEV, EXPERTS, TOPK, CAP, 2))(expert_ids_keys, expert_ids_turns).reshape((TOKENS, TOPK))
    gate_numer = place_ends(jax.random.randint(arg_keys[2], (TOKENS, TOPK), 8, 65), jax.random.fold_in(arg_keys[2], 1), 8, 64).astype(jnp.int32)
    gate_weight = normal_values(arg_keys[3], (EXPERTS, D, FF), D ** -0.5, 0.09375, ((0, 8), (2, 32)))
    up_weight = normal_values(arg_keys[4], (EXPERTS, D, FF), D ** -0.5, 0.09375, ((0, 8), (2, 32)))
    down_weight = normal_values(arg_keys[5], (EXPERTS, FF, D), FF ** -0.5, 0.046875, ((0, 8), (1, 32)))
    return dict(tokens=tokens, expert_ids=expert_ids, gate_numer=gate_numer, gate_weight=gate_weight, up_weight=up_weight, down_weight=down_weight)


def reference(tokens, expert_ids, gate_numer, gate_weight, up_weight, down_weight):
    rows = CAP * (TOKENS // TOK_DEV)
    pieces = N_EXPERT * N_HID
    width_piece = FF // pieces
    route_w = gate_numer.astype(jnp.float32) * (1.0 / 64.0)

    def one_expert(packed):
        index, w_gate, w_up, w_down = packed
        chosen = expert_ids == index
        picked = jnp.any(chosen, axis=1)
        scale = jnp.sum(jnp.where(chosen, route_w, jnp.float32(0.0)), axis=1)
        order = jnp.nonzero(picked, size=rows, fill_value=0)[0].astype(jnp.int32)
        live = (jnp.arange(rows, dtype=jnp.int32) < jnp.sum(picked.astype(jnp.int32))).astype(jnp.float32)
        rows_in = tokens[order]
        gate = jnp.dot(rows_in, w_gate, preferred_element_type=jnp.float32)
        upper = jnp.dot(rows_in, w_up, preferred_element_type=jnp.float32)
        hidden = (jax.nn.silu(gate) * upper).astype(jnp.bfloat16)
        hidden_parts = jnp.transpose(hidden.reshape(rows, pieces, width_piece), (1, 0, 2))
        down_parts = w_down.reshape(pieces, width_piece, D)

        def one_piece(carry, pair):
            left, right = pair
            partial_value = jnp.dot(left, right, preferred_element_type=jnp.float32).astype(jnp.bfloat16)
            partial_value = lax.optimization_barrier(partial_value).astype(jnp.float32)
            return carry + partial_value, None

        total, unused = lax.scan(one_piece, jnp.zeros((rows, D), jnp.float32), (hidden_parts, down_parts))
        result = total.astype(jnp.bfloat16)
        result = lax.optimization_barrier(result).astype(jnp.float32)
        factor = scale[order] * live
        return jnp.zeros((TOKENS, D), jnp.float32).at[order].add(result * factor[:, None])

    indices = jnp.arange(EXPERTS, dtype=jnp.int32)
    parts = lax.map(one_expert, (indices, gate_weight, up_weight, down_weight))
    return jnp.sum(parts, axis=0).astype(jnp.bfloat16)
```

```python
import functools

import jax
import jax.numpy as jnp
from jax import lax
from jax.experimental import pallas as pl
from jax.experimental.pallas import tpu as pltpu
from jax.sharding import PartitionSpec as P


CAP = 4


def shifted(x, axis, step):
    n = lax.axis_size(axis)
    return lax.ppermute(x, axis, [(i, (i + step) % n) for i in range(n)])


def joined(parts):
    return jnp.concatenate(parts, axis=0)


def added(*parts):
    total = parts[0].astype(jnp.float32)
    for part in parts[1:]:
        total = total + part.astype(jnp.float32)
    return total.astype(jnp.bfloat16)


def split_rows(x, count):
    rows = x.shape[0] // count
    return [x[i * rows:(i + 1) * rows] for i in range(count)]


def gather_eight(x):
    minus, plus = shifted(x, "expert", 1), shifted(x, "expert", -1)
    far = shifted(x, "expert", 4)
    below = shifted(joined([minus, far]), "expert", 1)
    above = shifted(joined([plus, far]), "expert", -1)
    return joined([x, minus, plus, far, below, above])


def scatter_eight(x):
    own, minus, plus, far, low, low_far, high, high_far = split_rows(x, 8)
    rows = own.shape[0]
    down = shifted(joined([low, low_far]), "expert", -1)
    up = shifted(joined([high, high_far]), "expert", 1)
    minus = shifted(added(minus, down[:rows]), "expert", -1)
    plus = shifted(added(plus, up[:rows]), "expert", 1)
    far = shifted(added(far, down[rows:], up[rows:]), "expert", 4)
    return added(own, minus, plus, far)


def gather_ring(x, axis):
    half = lax.axis_size(axis) // 2
    cut = x.shape[0] // 2
    parts = [x]
    fore, back = x, x
    for step in range(1, half + 1):
        if step == half:
            fore, back = fore[:cut], back[cut:]
        fore = shifted(fore, axis, 1)
        back = shifted(back, axis, -1)
        parts += [fore, back]
    return parts


def scatter_ring(blocks, axis):
    half = lax.axis_size(axis) // 2
    fore = shifted(blocks[-2], axis, 1)
    back = shifted(blocks[-1], axis, -1)
    for step in range(half - 1, 0, -1):
        minus, plus = blocks[2 * step - 1], blocks[2 * step]
        if step == half - 1:
            cut = fore.shape[0]
            plus = joined([added(plus[:cut], fore), plus[cut:]])
            minus = joined([minus[:cut], added(minus[cut:], back)])
        else:
            plus, minus = added(plus, fore), added(minus, back)
        fore = shifted(plus, axis, 1)
        back = shifted(minus, axis, -1)
    return added(blocks[0], fore, back)


def to_groups(rows):
    block = rows.reshape(lax.axis_size("group"), -1, rows.shape[-1])
    return lax.all_to_all(block, "group", split_axis=0, concat_axis=0, tiled=True).reshape(rows.shape)


def expert_kernel(count, *refs):
    parts, weights, outs = refs[:count], refs[count:count + 3], refs[count + 3:2 * count + 3]
    rows, held, hidden, sems = refs[2 * count + 3:]
    copies = [pltpu.make_async_copy(weights[i], held.at[i], sems.at[i]) for i in range(3)]
    for copy in copies:
        copy.start()
    at = 0
    for part in parts:
        rows[at:at + part.shape[0], :] = part[...]
        at += part.shape[0]
    by_columns = (((1,), (1,)), ((), ()))
    copies[0].wait()
    gate = lax.dot_general(rows[...], held[0], by_columns, preferred_element_type=jnp.float32)
    copies[1].wait()
    upper = lax.dot_general(rows[...], held[1], by_columns, preferred_element_type=jnp.float32)
    hidden[...] = (gate / (1.0 + jnp.exp(-gate)) * upper).astype(jnp.bfloat16)
    copies[2].wait()
    width = rows.shape[1]
    wide = min(1024, width)

    @pl.loop(0, width // wide)
    def _(i):
        columns = pl.ds(pl.multiple_of(i * wide, wide), wide)
        out = jnp.dot(hidden[...], held[2, :, columns], preferred_element_type=jnp.float32)
        out = out.astype(jnp.bfloat16)
        at = 0
        for ref in outs:
            ref[:, columns] = out[at:at + ref.shape[0]]
            at += ref.shape[0]


def expert_rows(parts, w_gate, w_up, w_down):
    total = sum(part.shape[0] for part in parts)
    units, width = w_down.shape
    in_vmem = pl.BlockSpec(memory_space=pltpu.VMEM)
    return pl.pallas_call(
        functools.partial(expert_kernel, len(parts)),
        out_shape=[jax.ShapeDtypeStruct(part.shape, part.dtype) for part in parts],
        in_specs=[in_vmem] * len(parts) + [pl.BlockSpec(memory_space=pl.ANY)] * 3,
        out_specs=[in_vmem] * len(parts),
        scratch_shapes=[
            pltpu.VMEM((total, width), jnp.bfloat16),
            pltpu.VMEM((3, units, width), jnp.bfloat16),
            pltpu.VMEM((total, units), jnp.bfloat16),
            pltpu.SemaphoreType.DMA((3,)),
        ],
        compiler_params=pltpu.CompilerParams(vmem_limit_bytes=40 * 2**20),
        cost_estimate=pl.CostEstimate(
            flops=6 * total * units * width,
            bytes_accessed=6 * units * width + 4 * total * width,
            transcendentals=total * units,
        ),
    )(*parts, w_gate, w_up, w_down)


def layer(tokens, expert_ids, gate_numer, gate_weight, up_weight, down_weight):
    tok, _ = tokens.shape
    experts = lax.axis_size("group")
    weights = gate_weight[0].T, up_weight[0].T, down_weight[0]

    hits = (expert_ids[:, :, None] == jnp.arange(experts, dtype=jnp.int32)).astype(jnp.float32)
    named = jnp.sum(hits, axis=1)
    share = jnp.sum(hits * (gate_numer.astype(jnp.float32) * (1.0 / 64.0))[:, :, None], axis=1)
    earlier = jnp.arange(tok)[:, None] > jnp.arange(tok)[None, :]
    rank = jnp.sum(jnp.where(earlier[:, :, None], named[None, :, :], 0.0), axis=1)
    at_slot = rank[:, :, None] == jnp.arange(CAP, dtype=jnp.float32)
    cells = experts * CAP
    take = jnp.where(at_slot, named[:, :, None], 0.0).astype(jnp.bfloat16).reshape(tok, cells)
    mix = jnp.where(at_slot, share[:, :, None], 0.0).astype(jnp.bfloat16).reshape(tok, cells)

    outgoing = jnp.dot(take.T, tokens, preferred_element_type=jnp.float32).astype(jnp.bfloat16)
    arrived = to_groups(outgoing)
    half_a, half_b = split_rows(arrived, 2)

    parts_y = gather_ring(gather_eight(half_b), "hid")
    minus, plus = shifted(half_a, "hid", 1), shifted(half_a, "hid", -1)
    far = shifted(half_a, "hid", 2)
    parts_0 = gather_ring(joined([half_a, minus]), "expert")
    parts_1 = gather_ring(joined([plus, far]), "expert")

    near_a = expert_rows(parts_0[:5] + parts_1[:5], *weights)
    near_a, parts_y[:3] = lax.optimization_barrier((near_a, parts_y[:3]))
    near_y = expert_rows(parts_y[:3], *weights)
    last = parts_y[3:] + parts_0[5:] + parts_1[5:]
    near_y, last = lax.optimization_barrier((near_y, last))
    last = expert_rows(last, *weights)

    home_0 = scatter_ring(near_a[:5] + last[2:6], "expert")
    home_1 = scatter_ring(near_a[5:] + last[6:], "expert")
    home_b = scatter_eight(scatter_ring(near_y + last[:2], "hid"))
    own, minus = split_rows(home_0, 2)
    plus, far = split_rows(home_1, 2)
    home_a = added(own, shifted(minus, "hid", -1), shifted(plus, "hid", 1), shifted(far, "hid", 2))
    returned = to_groups(joined([home_a, home_b]))
    return jnp.dot(mix, returned, preferred_element_type=jnp.float32).astype(jnp.bfloat16)


def solution(mesh):
    return jax.shard_map(
        layer,
        mesh=mesh,
        in_specs=(
            P(("group", "expert", "hid"), None),
            P(("group", "expert", "hid"), None),
            P(("group", "expert", "hid"), None),
            P("group", None, ("expert", "hid")),
            P("group", None, ("expert", "hid")),
            P("group", ("expert", "hid"), None),
        ),
        out_specs=P(("group", "expert", "hid"), None),
        check_vma=False,
    )
```

```python
import functools

import jax
import jax.numpy as jnp
from jax import lax
from jax.experimental import pallas as pl
from jax.experimental.pallas import tpu as pltpu
from jax.sharding import PartitionSpec as P


CAP = 4


def shifted(x, axis, step):
    n = lax.axis_size(axis)
    return lax.ppermute(x, axis, [(i, (i + step) % n) for i in range(n)])


def joined(parts):
    return jnp.concatenate(parts, axis=0)


def added(*parts):
    total = parts[0].astype(jnp.float32)
    for part in parts[1:]:
        total = total + part.astype(jnp.float32)
    return total.astype(jnp.bfloat16)


def split_rows(x, count):
    rows = x.shape[0] // count
    return [x[i * rows:(i + 1) * rows] for i in range(count)]


def gather_eight(x):
    minus, plus = shifted(x, "expert", 1), shifted(x, "expert", -1)
    far = shifted(x, "expert", 4)
    below = shifted(joined([minus, far]), "expert", 1)
    above = shifted(joined([plus, far]), "expert", -1)
    return joined([x, minus, plus, far, below, above])


def scatter_eight(x):
    own, minus, plus, far, low, low_far, high, high_far = split_rows(x, 8)
    rows = own.shape[0]
    down = shifted(joined([low, low_far]), "expert", -1)
    up = shifted(joined([high, high_far]), "expert", 1)
    minus = shifted(added(minus, down[:rows]), "expert", -1)
    plus = shifted(added(plus, up[:rows]), "expert", 1)
    far = shifted(added(far, down[rows:], up[rows:]), "expert", 4)
    return added(own, minus, plus, far)


def gather_ring(x, axis):
    half = lax.axis_size(axis) // 2
    cut = x.shape[0] // 2
    parts = [x]
    fore, back = x, x
    for step in range(1, half + 1):
        if step == half:
            fore, back = fore[:cut], back[cut:]
        fore = shifted(fore, axis, 1)
        back = shifted(back, axis, -1)
        parts += [fore, back]
    return parts


def scatter_ring(blocks, axis):
    half = lax.axis_size(axis) // 2
    fore = shifted(blocks[-2], axis, 1)
    back = shifted(blocks[-1], axis, -1)
    for step in range(half - 1, 0, -1):
        minus, plus = blocks[2 * step - 1], blocks[2 * step]
        if step == half - 1:
            cut = fore.shape[0]
            plus = joined([added(plus[:cut], fore), plus[cut:]])
            minus = joined([minus[:cut], added(minus[cut:], back)])
        else:
            plus, minus = added(plus, fore), added(minus, back)
        fore = shifted(plus, axis, 1)
        back = shifted(minus, axis, -1)
    return added(blocks[0], fore, back)


def to_groups(rows):
    block = rows.reshape(lax.axis_size("group"), -1, rows.shape[-1])
    return lax.all_to_all(block, "group", split_axis=0, concat_axis=0, tiled=True).reshape(rows.shape)


def expert_kernel(count, *refs):
    parts, weights, outs = refs[:count], refs[count:count + 3], refs[count + 3:2 * count + 3]
    rows, held, hidden, sems = refs[2 * count + 3:]
    copies = [pltpu.make_async_copy(weights[i], held.at[i], sems.at[i]) for i in range(3)]
    for copy in copies:
        copy.start()
    at = 0
    for part in parts:
        rows[at:at + part.shape[0], :] = part[...]
        at += part.shape[0]
    by_columns = (((1,), (1,)), ((), ()))
    copies[0].wait()
    gate = lax.dot_general(rows[...], held[0], by_columns, preferred_element_type=jnp.float32)
    copies[1].wait()
    upper = lax.dot_general(rows[...], held[1], by_columns, preferred_element_type=jnp.float32)
    hidden[...] = (gate / (1.0 + jnp.exp(-gate)) * upper).astype(jnp.bfloat16)
    copies[2].wait()
    width = rows.shape[1]
    wide = min(512, width)

    @pl.loop(0, width // wide)
    def _(i):
        columns = pl.ds(pl.multiple_of(i * wide, wide), wide)
        out = jnp.dot(hidden[...], held[2, :, columns], preferred_element_type=jnp.float32)
        out = out.astype(jnp.bfloat16)
        at = 0
        for ref in outs:
            ref[:, columns] = out[at:at + ref.shape[0]]
            at += ref.shape[0]


def expert_rows(parts, w_gate, w_up, w_down):
    total = sum(part.shape[0] for part in parts)
    units, width = w_down.shape
    in_vmem = pl.BlockSpec(memory_space=pltpu.VMEM)
    return pl.pallas_call(
        functools.partial(expert_kernel, len(parts)),
        out_shape=[jax.ShapeDtypeStruct(part.shape, part.dtype) for part in parts],
        in_specs=[in_vmem] * len(parts) + [pl.BlockSpec(memory_space=pl.ANY)] * 3,
        out_specs=[in_vmem] * len(parts),
        scratch_shapes=[
            pltpu.VMEM((total, width), jnp.bfloat16),
            pltpu.VMEM((3, units, width), jnp.bfloat16),
            pltpu.VMEM((total, units), jnp.bfloat16),
            pltpu.SemaphoreType.DMA((3,)),
        ],
        compiler_params=pltpu.CompilerParams(vmem_limit_bytes=44 * 2**20),
        cost_estimate=pl.CostEstimate(
            flops=6 * total * units * width,
            bytes_accessed=6 * units * width + 4 * total * width,
            transcendentals=total * units,
        ),
    )(*parts, w_gate, w_up, w_down)


def layer(tokens, expert_ids, gate_numer, gate_weight, up_weight, down_weight):
    tok, _ = tokens.shape
    experts = lax.axis_size("group")
    weights = gate_weight[0].T, up_weight[0].T, down_weight[0]

    hits = (expert_ids[:, :, None] == jnp.arange(experts, dtype=jnp.int32)).astype(jnp.float32)
    named = jnp.sum(hits, axis=1)
    share = jnp.sum(hits * (gate_numer.astype(jnp.float32) * (1.0 / 64.0))[:, :, None], axis=1)
    earlier = jnp.arange(tok)[:, None] > jnp.arange(tok)[None, :]
    rank = jnp.sum(jnp.where(earlier[:, :, None], named[None, :, :], 0.0), axis=1)
    at_slot = rank[:, :, None] == jnp.arange(CAP, dtype=jnp.float32)
    cells = experts * CAP
    take = jnp.where(at_slot, named[:, :, None], 0.0).astype(jnp.bfloat16).reshape(tok, cells)
    mix = jnp.where(at_slot, share[:, :, None], 0.0).astype(jnp.bfloat16).reshape(tok, cells)

    outgoing = jnp.dot(take.T, tokens, preferred_element_type=jnp.float32).astype(jnp.bfloat16)
    arrived = to_groups(outgoing)
    half_a, half_b = split_rows(arrived, 2)

    parts_y = gather_ring(gather_eight(half_b), "hid")
    minus, plus = shifted(half_a, "hid", 1), shifted(half_a, "hid", -1)
    far = shifted(half_a, "hid", 2)
    parts_0 = gather_ring(joined([half_a, minus]), "expert")
    parts_1 = gather_ring(joined([plus, far]), "expert")

    near_a = expert_rows(parts_0[:5] + parts_1[:5], *weights)
    last = parts_y + parts_0[5:] + parts_1[5:]
    near_a, last = lax.optimization_barrier((near_a, last))
    last = expert_rows(last, *weights)

    home_0 = scatter_ring(near_a[:5] + last[5:9], "expert")
    home_1 = scatter_ring(near_a[5:] + last[9:], "expert")
    home_b = scatter_eight(scatter_ring(last[:5], "hid"))
    own, minus = split_rows(home_0, 2)
    plus, far = split_rows(home_1, 2)
    home_a = added(own, shifted(minus, "hid", -1), shifted(plus, "hid", 1), shifted(far, "hid", 2))
    returned = to_groups(joined([home_a, home_b]))
    return jnp.dot(mix, returned, preferred_element_type=jnp.float32).astype(jnp.bfloat16)


def solution(mesh):
    return jax.shard_map(
        layer,
        mesh=mesh,
        in_specs=(
            P(("group", "expert", "hid"), None),
            P(("group", "expert", "hid"), None),
            P(("group", "expert", "hid"), None),
            P("group", None, ("expert", "hid")),
            P("group", None, ("expert", "hid")),
            P("group", ("expert", "hid"), None),
        ),
        out_specs=P(("group", "expert", "hid"), None),
        check_vma=False,
    )
```

```python
import functools

import jax
import jax.numpy as jnp
from jax import lax
from jax.experimental import pallas as pl
from jax.experimental.pallas import tpu as pltpu
from jax.sharding import PartitionSpec as P


CAP = 4


def shifted(x, axis, step):
    n = lax.axis_size(axis)
    return lax.ppermute(x, axis, [(i, (i + step) % n) for i in range(n)])


def joined(parts):
    return jnp.concatenate(parts, axis=0)


def added(*parts):
    total = parts[0].astype(jnp.float32)
    for part in parts[1:]:
        total = total + part.astype(jnp.float32)
    return total.astype(jnp.bfloat16)


def split_rows(x, count):
    rows = x.shape[0] // count
    return [x[i * rows:(i + 1) * rows] for i in range(count)]


def gather_eight(x):
    minus, plus = shifted(x, "expert", 1), shifted(x, "expert", -1)
    far = shifted(x, "expert", 4)
    below = shifted(joined([minus, far]), "expert", 1)
    above = shifted(joined([plus, far]), "expert", -1)
    return joined([x, minus, plus, far, below, above])


def scatter_eight(x):
    own, minus, plus, far, low, low_far, high, high_far = split_rows(x, 8)
    rows = own.shape[0]
    down = shifted(joined([low, low_far]), "expert", -1)
    up = shifted(joined([high, high_far]), "expert", 1)
    minus = shifted(added(minus, down[:rows]), "expert", -1)
    plus = shifted(added(plus, up[:rows]), "expert", 1)
    far = shifted(added(far, down[rows:], up[rows:]), "expert", 4)
    return added(own, minus, plus, far)


def gather_ring(x, axis, way="both"):
    half = lax.axis_size(axis) // 2
    cut = x.shape[0] // 2
    parts = [x]
    fore, back = x, x
    for step in range(1, half + 1):
        last = step == half
        if last and way == "both":
            fore, back = fore[:cut], back[cut:]
        if not last or way != "back":
            fore = shifted(fore, axis, 1)
            parts.append(fore)
        if not last or way != "fore":
            back = shifted(back, axis, -1)
            parts.append(back)
    return parts


def scatter_ring(blocks, axis, way="both"):
    half = lax.axis_size(axis) // 2
    fore = back = None
    if way != "back":
        fore = shifted(blocks[2 * half - 1], axis, 1)
    if way != "fore":
        back = shifted(blocks[-1], axis, -1)
    for step in range(half - 1, 0, -1):
        minus, plus = blocks[2 * step - 1], blocks[2 * step]
        if step == half - 1 and way == "both":
            cut = fore.shape[0]
            plus = joined([added(plus[:cut], fore), plus[cut:]])
            minus = joined([minus[:cut], added(minus[cut:], back)])
        else:
            plus = plus if fore is None else added(plus, fore)
            minus = minus if back is None else added(minus, back)
        fore = shifted(plus, axis, 1)
        back = shifted(minus, axis, -1)
    return added(blocks[0], fore, back)


def to_groups(rows):
    block = rows.reshape(lax.axis_size("group"), -1, rows.shape[-1])
    return lax.all_to_all(block, "group", split_axis=0, concat_axis=0, tiled=True).reshape(rows.shape)


def expert_kernel(count, *refs):
    parts, weights, outs = refs[:count], refs[count:count + 3], refs[count + 3:2 * count + 3]
    rows, held, hidden, sems = refs[2 * count + 3:]
    copies = [pltpu.make_async_copy(weights[i], held.at[i], sems.at[i]) for i in range(3)]
    for copy in copies:
        copy.start()
    at = 0
    for part in parts:
        rows[at:at + part.shape[0], :] = part[...]
        at += part.shape[0]
    by_columns = (((1,), (1,)), ((), ()))
    copies[0].wait()
    gate = lax.dot_general(rows[...], held[0], by_columns, preferred_element_type=jnp.float32)
    copies[1].wait()
    upper = lax.dot_general(rows[...], held[1], by_columns, preferred_element_type=jnp.float32)
    hidden[...] = (gate / (1.0 + jnp.exp(-gate)) * upper).astype(jnp.bfloat16)
    copies[2].wait()
    width = rows.shape[1]
    wide = min(512, width)

    @pl.loop(0, width // wide)
    def _(i):
        columns = pl.ds(pl.multiple_of(i * wide, wide), wide)
        out = jnp.dot(hidden[...], held[2, :, columns], preferred_element_type=jnp.float32)
        out = out.astype(jnp.bfloat16)
        at = 0
        for ref in outs:
            ref[:, columns] = out[at:at + ref.shape[0]]
            at += ref.shape[0]


def expert_rows(parts, w_gate, w_up, w_down):
    total = sum(part.shape[0] for part in parts)
    units, width = w_down.shape
    in_vmem = pl.BlockSpec(memory_space=pltpu.VMEM)
    return pl.pallas_call(
        functools.partial(expert_kernel, len(parts)),
        out_shape=[jax.ShapeDtypeStruct(part.shape, part.dtype) for part in parts],
        in_specs=[in_vmem] * len(parts) + [pl.BlockSpec(memory_space=pl.ANY)] * 3,
        out_specs=[in_vmem] * len(parts),
        scratch_shapes=[
            pltpu.VMEM((total, width), jnp.bfloat16),
            pltpu.VMEM((3, units, width), jnp.bfloat16),
            pltpu.VMEM((total, units), jnp.bfloat16),
            pltpu.SemaphoreType.DMA((3,)),
        ],
        compiler_params=pltpu.CompilerParams(vmem_limit_bytes=44 * 2**20),
        cost_estimate=pl.CostEstimate(
            flops=6 * total * units * width,
            bytes_accessed=6 * units * width + 4 * total * width,
            transcendentals=total * units,
        ),
    )(*parts, w_gate, w_up, w_down)


def layer(tokens, expert_ids, gate_numer, gate_weight, up_weight, down_weight):
    tok, _ = tokens.shape
    experts = lax.axis_size("group")
    weights = gate_weight[0].T, up_weight[0].T, down_weight[0]

    hits = (expert_ids[:, :, None] == jnp.arange(experts, dtype=jnp.int32)).astype(jnp.float32)
    named = jnp.sum(hits, axis=1)
    share = jnp.sum(hits * (gate_numer.astype(jnp.float32) * (1.0 / 64.0))[:, :, None], axis=1)
    earlier = jnp.arange(tok)[:, None] > jnp.arange(tok)[None, :]
    rank = jnp.sum(jnp.where(earlier[:, :, None], named[None, :, :], 0.0), axis=1)
    at_slot = rank[:, :, None] == jnp.arange(CAP, dtype=jnp.float32)
    cells = experts * CAP
    take = jnp.where(at_slot, named[:, :, None], 0.0).astype(jnp.bfloat16).reshape(tok, cells)
    mix = jnp.where(at_slot, share[:, :, None], 0.0).astype(jnp.bfloat16).reshape(tok, cells)

    outgoing = jnp.dot(take.T, tokens, preferred_element_type=jnp.float32).astype(jnp.bfloat16)
    arrived = to_groups(outgoing)
    half_a, half_b = split_rows(arrived, 2)

    parts_y = gather_ring(gather_eight(half_b), "hid")
    minus, plus = shifted(half_a, "hid", 1), shifted(half_a, "hid", -1)
    far = shifted(half_a, "hid", 2)
    parts_0 = gather_ring(joined([half_a, minus]), "expert", "fore")
    parts_1 = gather_ring(joined([plus, far]), "expert", "back")

    near_a = expert_rows(parts_0[:5] + parts_1[:5], *weights)
    last = parts_y + parts_0[5:] + parts_1[5:]
    near_a, last = lax.optimization_barrier((near_a, last))
    last = expert_rows(last, *weights)

    home_0 = scatter_ring(near_a[:5] + last[5:8], "expert", "fore")
    home_1 = scatter_ring(near_a[5:] + last[8:], "expert", "back")
    home_b = scatter_eight(scatter_ring(last[:5], "hid"))
    own, minus = split_rows(home_0, 2)
    plus, far = split_rows(home_1, 2)
    home_a = added(own, shifted(minus, "hid", -1), shifted(plus, "hid", 1), shifted(far, "hid", 2))
    returned = to_groups(joined([home_a, home_b]))
    return jnp.dot(mix, returned, preferred_element_type=jnp.float32).astype(jnp.bfloat16)


def solution(mesh):
    return jax.shard_map(
        layer,
        mesh=mesh,
        in_specs=(
            P(("group", "expert", "hid"), None),
            P(("group", "expert", "hid"), None),
            P(("group", "expert", "hid"), None),
            P("group", None, ("expert", "hid")),
            P("group", None, ("expert", "hid")),
            P("group", ("expert", "hid"), None),
        ),
        out_specs=P(("group", "expert", "hid"), None),
        check_vma=False,
    )
```
